32 devices in a mesh: group: 2 (over x), row: 8 (over z, y), tp: 2 (over core).
Axes of the slice: x: 2, y: 2, z: 4, core: 2. Of those that a mesh axis runs over, the one named last changes fastest.
Arguments:
- prompt_latent: bfloat16 [16, 16, 128, 576], P(('group', 'row'), None, 'tp'), parts along dimension 0, may hold values from -6 to 6
- row_cache: bfloat16 [32, 256, 576], P(('group', 'row')), parts along dimension 0, may hold values from -24 to 24
- queries: bfloat16 [4, 32, 128, 576], P(None, ('group', 'row'), 'tp'), parts along dimension 1, may hold values from -80 to 80
- new_latent: bfloat16 [4, 32, 576], P(None, ('group', 'row')), parts along dimension 1, may hold values from -12 to 12
- prompt_len: int32 [32], P('group'), parts along dimension 0, may hold values from 1 to 1024, 12288 in all
- assign: int32 [32], P('group'), parts along dimension 0, may hold values from 0 to 15, as said below
- row_ctx: int32 [32], P(('group', 'row')), parts along dimension 0, may hold values from 2 to 256
Outputs:
- attended: bfloat16 [4, 32, 128, 512], P(None, ('group', 'row'), 'tp'), parts along dimension 1
The draws below stay inside these ranges and needn't reach their ends.
There are 2 independent parts, one for each index of `group`. The reference program is written for one: setup_inputs(seed, part) draws one part's arguments, and reference() takes and returns one part's arrays. A program takes and returns all parts, laid end to end along the dimension named above; each array names one. Nothing has to cross between parts.
Inputs may be any that keep to these rules, and one draw needn't show every extreme that they name: `prompt_len`: latents at positions from a prompt's length on are not part of that prompt. Decode row r continues prompt assign[r]; every prompt goes to exactly one row. Prompt p belongs to prompt group p // 16; the rows of one index of row take at most 2 prompts of any one prompt group. Row r's cached latents are its first row_ctx[r] positions.
All inputs are finite; a program needn't handle non-finite values.
Results may differ from the reference program's by a relative error of at most 0.0044.
Values may be sent and summed in bfloat16 or wider, within the bound.
No kernel may reach another device: no remote copies, remote signals or barrier semaphores. Data moves between devices by JAX's collectives and lax.ppermute only.
A program may use at most 128 MiB of HBM per device.

```python
import math
import jax
import jax.numpy as jnp
import numpy as np
from jax import lax

HEADS = 128
KV_RANK = 512
ROPE_DIM = 64
NOPE_DIM = 128
ROWS_DEV = 2
LMAX = 1024
CMAX = 256
STEPS = 4
SPR = 8
ROWS = 16
MOST = 2
N_ROW = 8


def joint_rows(key):
    base_key = jax.random.fold_in(key, 4242)
    key_cache, key_query = jax.random.split(base_key, 2)
    latent_width = KV_RANK + ROPE_DIM
    cache_rows = jnp.clip(jax.random.normal(key_cache, (ROWS, CMAX, latent_width), jnp.float32), -6.0, 6.0)
    query_rows = 1.5 * jnp.clip(jax.random.normal(key_query, (STEPS, ROWS, HEADS, latent_width), jnp.float32), -6.0, 6.0)
    return (cache_rows, query_rows)


def draw_row_cache(key, part):
    return joint_rows(key)[0].astype(jnp.bfloat16)


def draw_queries(key, part):
    return joint_rows(key)[1].astype(jnp.bfloat16)


def draw_assign(key, part):
    base_key = jax.random.fold_in(key, 7717)
    key_anchor, key_blocks, key_slots, key_order = jax.random.split(base_key, 4)
    group_total = N_ROW // SPR
    block_total = ROWS_DEV // MOST
    stride_groups = group_total // block_total
    anchor = jax.random.randint(key_anchor, (), 0, N_ROW).astype(jnp.int32)
    block_keys = jax.random.split(key_blocks, block_total)
    slot_keys = jax.random.split(key_slots, ROWS_DEV)
    devices = jnp.arange(N_ROW, dtype=jnp.int32)
    relative = (devices - anchor) % N_ROW
    columns = []
    for slot_id in range(ROWS_DEV):
        block_id = slot_id // MOST
        block_perm = jax.random.permutation(block_keys[block_id], N_ROW).astype(jnp.int32)
        others = 1 + jax.random.permutation(slot_keys[slot_id], N_ROW - 1).astype(jnp.int32)
        fixed_first = jnp.concatenate([jnp.zeros((1,), jnp.int32), others], 0)
        moved_device = (jnp.take(fixed_first, relative) + anchor) % N_ROW
        chosen = jnp.take(block_perm, moved_device)
        columns.append(chosen % stride_groups * block_total + block_id)
    group_label = jnp.stack(columns, 1).reshape(ROWS).astype(jnp.int32)
    order_key = group_label * ROWS + jax.random.permutation(key_order, ROWS).astype(jnp.int32)
    order = jnp.argsort(order_key)
    return jnp.zeros((ROWS,), jnp.int32).at[order].set(jnp.arange(ROWS, dtype=jnp.int32))


def with_ends(array, key, smallest, largest):
    longest = array.shape.index(max(array.shape))
    spots = []
    for shift in (0, 1):
        where = [jax.random.randint(jax.random.fold_in(key, axis), (), 0, length) for axis, length in enumerate(array.shape)]
        where[longest] = (where[longest] + shift) % array.shape[longest]
        spots.append(tuple(where))
    return array.at[spots[0]].set(smallest).at[spots[1]].set(largest)


def block_levels(rng, shape, cuts, least, top_value):
    gain = 1.0
    for dim, parts in cuts:
        steps = jax.random.uniform(jax.random.fold_in(jax.random.fold_in(rng, 6), dim), (parts,), jnp.float32, least / len(cuts), top_value / len(cuts))
        gain = gain * jnp.repeat(jnp.exp(steps), shape[dim] // parts).reshape((-1,) + (1,) * (len(shape) - 1 - dim))
    return gain


def split_up(count, total, reach, skew):
    loads = [(1 << 20) // math.isqrt(standing ** skew) + 1 for standing in range(2, count + 1)]
    spare, holding = total - reach - (count - 1), [1] * (count - 1)
    while spare > 0:
        free = [i for i in range(count - 1) if holding[i] < reach]
        mass, budget = sum([loads[i] for i in free]), spare
        for i in free:
            extra = min(reach - holding[i], max(1, budget * loads[i] // mass), spare)
            holding[i] = holding[i] + extra
            spare = spare - extra
    return np.array([reach] + holding)


def uneven(stream_key, count, total, bound, slope):
    if count == 2:
        one = jax.random.randint(stream_key, (), max(1, total - bound), min(bound, total - 1) + 1)
        return jnp.stack([one, total - one])
    sizes = jnp.asarray(split_up(count, total, bound, slope), jnp.int32)
    couples = (count - 1) // 2
    source_of, sink = sizes[1:1 + 2 * couples:2], sizes[2:2 + 2 * couples:2]
    margin = jnp.minimum(source_of - 1, bound - sink)
    moved = jax.random.randint(jax.random.fold_in(stream_key, 1), (couples,), 0, 1 << 20) % (margin + 1)
    sizes = sizes.at[1:1 + 2 * couples:2].set(source_of - moved).at[2:2 + 2 * couples:2].set(sink + moved)
    return sizes[jax.random.permutation(jax.random.fold_in(stream_key, 2), count)]


def noise(key, extent, scale, reach, cuts=(), held_as=jnp.bfloat16):
    drawn = jax.random.normal(key, extent, jnp.float32) * scale
    if len(cuts) > 0:
        drawn = block_levels(key, extent, cuts, -0.22, 0.18) * drawn
    return jnp.clip(drawn, min=-reach, max=reach).astype(held_as)


def setup_inputs(seed: int = 0, part: int = 0) -> dict:
    key_list = jax.random.split(jax.random.key(seed), 8)
    own_keys = jax.random.split(jax.random.fold_in(key_list[7], part), 8)
    prompt_latent = noise(own_keys[0], (N_ROW, ROWS_DEV * SPR, LMAX // SPR, KV_RANK + ROPE_DIM), 1.0, 6.0, ((0, 8), (2, 2)))
    row_cache = draw_row_cache(jax.random.fold_in(jax.random.fold_in(key_list[7], part), 71), part)
    queries = draw_queries(jax.random.fold_in(jax.random.fold_in(key_list[7], part), 71), part)
    new_latent = noise(own_keys[3], (STEPS, ROWS, KV_RANK + ROPE_DIM), 2.0, 12.0, ((1, 8),))
    prompt_len = uneven(own_keys[4], ROWS, ROWS * LMAX * 3 // 4, LMAX, 2).astype(jnp.int32)
    assign = draw_assign(jax.random.fold_in(jax.random.fold_in(key_list[7], part), 71), part)
    row_ctx = with_ends(jax.random.randint(own_keys[6], (ROWS,), 2, CMAX + 1), jax.random.fold_in(own_keys[6], 1), 2, CMAX).astype(jnp.int32)
    return {"prompt_latent": prompt_latent, "row_cache": row_cache, "queries": queries, "new_latent": new_latent, "prompt_len": prompt_len, "assign": assign, "row_ctx": row_ctx}


def reference(prompt_latent, row_cache, queries, new_latent, prompt_len, assign, row_ctx):
    scale_factor = (NOPE_DIM + ROPE_DIM) ** -0.5
    steps_idx = jnp.arange(STEPS, dtype=jnp.int32)
    causal = steps_idx[None, :] <= steps_idx[:, None]
    group_rows = ROWS_DEV * SPR
    latent_width = KV_RANK + ROPE_DIM
    zero_index = jnp.zeros((), jnp.int32)

    def one_row(row_index):
        prompt_id = assign[row_index].astype(jnp.int32)
        group_id = (prompt_id // group_rows).astype(jnp.int32)
        inner_id = (prompt_id - group_id * group_rows).astype(jnp.int32)
        prompt_keys = lax.dynamic_slice(prompt_latent, (group_id * SPR, inner_id, zero_index, zero_index),
                                        (SPR, 1, LMAX // SPR, latent_width)).reshape(LMAX, latent_width)
        live_len = lax.dynamic_index_in_dim(prompt_len, prompt_id, 0, keepdims=False)
        cache_keys = lax.dynamic_index_in_dim(row_cache, row_index, 0, keepdims=False)
        cache_len = lax.dynamic_index_in_dim(row_ctx, row_index, 0, keepdims=False)
        query_rows = lax.dynamic_index_in_dim(queries, row_index, 1, keepdims=False)
        fresh_keys = lax.dynamic_index_in_dim(new_latent, row_index, 1, keepdims=False)
        all_keys = jnp.concatenate([prompt_keys, cache_keys, fresh_keys], 0).astype(jnp.float32)
        scores = jnp.einsum("shc,kc->shk", query_rows.astype(jnp.float32), all_keys) * scale_factor
        prompt_mask = jnp.arange(LMAX, dtype=jnp.int32) < live_len
        cache_mask = jnp.arange(CMAX, dtype=jnp.int32) < cache_len
        full_mask = jnp.concatenate([jnp.broadcast_to(prompt_mask[None, :], (STEPS, LMAX)),
                                     jnp.broadcast_to(cache_mask[None, :], (STEPS, CMAX)), causal], 1)
        scores = jnp.where(full_mask[:, None, :], scores, -jnp.inf)
        row_top = jnp.max(scores, axis=2, keepdims=True)
        exponent = jnp.exp(scores - row_top)
        weights = (exponent / jnp.sum(exponent, axis=2, keepdims=True)).astype(jnp.bfloat16)
        values = all_keys[:, :KV_RANK]
        return jnp.einsum("shk,kc->shc", weights.astype(jnp.float32), values).astype(jnp.bfloat16)

    result = lax.map(one_row, jnp.arange(ROWS, dtype=jnp.int32))
    return jnp.transpose(result, (1, 0, 2, 3))
```

```python
import functools

import jax
import jax.numpy as jnp
from jax import lax
from jax.experimental import pallas as pl
from jax.experimental.pallas import tpu as pltpu
from jax.sharding import PartitionSpec as P


KV_RANK = 512
ROPE_DIM = 64
NOPE_DIM = 128
SPR = 8


PACK_VMEM = 4 << 20
ATTEND_VMEM = 16 << 20

SEND_ORDER = (7, 6, 5, 4, 3, 2, 1)
STAGES = ((0,), (1, 2, 3), (7, 6), (5, 4))


def pack_kernel(order, assign_ref, place_ref, latent_ref, *refs):
    outs, sems = refs[:-1], refs[-1]
    rows_here = outs[0].shape[0]
    place = place_ref[0]
    copies = []
    for i, offset in enumerate(order):
        for slot in range(rows_here):
            prompt = assign_ref[(place ^ offset) * rows_here + slot]
            copy = pltpu.make_async_copy(
                latent_ref.at[prompt], outs[i].at[slot], sems.at[i, slot]
            )
            copy.start()
            copies.append(copy)
    for copy in copies:
        copy.wait()


def pack(order, assign, place, local, rows_here):
    shape = (rows_here,) + local.shape[1:]
    return pl.pallas_call(
        functools.partial(pack_kernel, order),
        out_shape=[jax.ShapeDtypeStruct(shape, local.dtype) for _ in order],
        in_specs=[
            pl.BlockSpec(memory_space=pltpu.SMEM),
            pl.BlockSpec(memory_space=pltpu.SMEM),
            pl.BlockSpec(memory_space=pl.ANY),
        ],
        out_specs=[pl.BlockSpec(memory_space=pltpu.VMEM) for _ in order],
        scratch_shapes=[pltpu.SemaphoreType.DMA((len(order), rows_here))],
        compiler_params=pltpu.CompilerParams(vmem_limit_bytes=PACK_VMEM),
        name="pack",
    )(assign, place.reshape(1), local)


def attend_kernel(offsets, first, last, info_ref, q_ref, *refs):
    refs = list(refs)
    own = [refs.pop(0) for _ in offsets]
    other = [refs.pop(0) for _ in offsets]
    if first:
        cache_ref, new_ref = refs.pop(0), refs.pop(0)
    else:
        top_in, sum_in, acc_in = refs.pop(0), refs.pop(0), refs.pop(0)
    if last:
        out_ref = refs.pop(0)
    else:
        top_out, sum_out, acc_out = refs.pop(0), refs.pop(0), refs.pop(0)
    keys_ref = refs.pop(0)
    steps, rows, heads, width = q_ref.shape
    piece = own[0].shape[1]
    block = 2 * piece
    scale = (NOPE_DIM + ROPE_DIM) ** -0.5
    place, side = info_ref[2 * rows], info_ref[2 * rows + 1]
    for r in range(rows):
        used = 0
        masks = []
        live = info_ref[r]
        for i, offset in enumerate(offsets):
            keys_ref[r, used : used + piece] = own[i][r]
            keys_ref[r, used + piece : used + block] = other[i][r]
            lane = lax.broadcasted_iota(jnp.int32, (1, block), 1)
            flip = jnp.where(lane < piece, side, 1 - side) * piece + lane % piece
            masks.append((place ^ offset) * block + flip < live)
            used += block
        if first:
            cached = cache_ref.shape[1]
            keys_ref[r, used : used + cached] = cache_ref[r]
            lane = lax.broadcasted_iota(jnp.int32, (1, cached), 1)
            masks.append(lane < info_ref[rows + r])
            used += cached
        key = keys_ref[r, :used]
        query = q_ref[:, r].reshape(steps * heads, width)
        contract = (((1,), (1,)), ((), ()))
        scores = lax.dot_general(query, key, contract, preferred_element_type=jnp.float32)
        scores = jnp.where(jnp.concatenate(masks, axis=1), scores * scale, -jnp.inf)
        top = jnp.max(scores, axis=1, keepdims=True)
        if first:
            fresh_key = new_ref[r]
            fresh = lax.dot_general(query, fresh_key, contract, preferred_element_type=jnp.float32)
            step = lax.broadcasted_iota(jnp.int32, fresh.shape, 0) // heads
            slot = lax.broadcasted_iota(jnp.int32, fresh.shape, 1)
            fresh = jnp.where(slot <= step, fresh * scale, -jnp.inf)
            top = jnp.maximum(top, jnp.max(fresh, axis=1, keepdims=True))
        else:
            top = jnp.maximum(top, top_in[r])
        weight = jnp.exp(scores - top)
        total = jnp.sum(weight, axis=1, keepdims=True)
        acc = jnp.dot(
            weight.astype(key.dtype), key[:, :KV_RANK], preferred_element_type=jnp.float32
        )
        if first:
            fresh_weight = jnp.exp(fresh - top)
            total += jnp.sum(fresh_weight, axis=1, keepdims=True)
            acc += jnp.dot(
                fresh_weight.astype(key.dtype),
                fresh_key[:, :KV_RANK],
                preferred_element_type=jnp.float32,
            )
        else:
            shrink = jnp.exp(top_in[r] - top)
            total += shrink * sum_in[r]
            acc += shrink * acc_in[r]
        if last:
            out = (acc / total).astype(out_ref.dtype)
            out_ref[:, r] = out.reshape(steps, heads, KV_RANK)
        else:
            top_out[r] = top
            sum_out[r] = total
            acc_out[r] = acc


def attend(offsets, info, queries, own, other, cache=None, fresh=None, carry=None, last=False):
    steps, rows, heads, width = queries.shape
    first = carry is None
    keys = 2 * own[0].shape[1] * len(offsets) + (cache.shape[1] if first else 0)
    tall = steps * heads
    state = (
        jax.ShapeDtypeStruct((rows, tall, 1), jnp.float32),
        jax.ShapeDtypeStruct((rows, tall, 1), jnp.float32),
        jax.ShapeDtypeStruct((rows, tall, KV_RANK), jnp.float32),
    )
    out_shape = jax.ShapeDtypeStruct((steps, rows, heads, KV_RANK), queries.dtype) if last else state
    extra = (cache, fresh) if first else carry
    operands = (info, queries, *own, *other, *extra)
    vmem = pl.BlockSpec(memory_space=pltpu.VMEM)
    return pl.pallas_call(
        functools.partial(attend_kernel, offsets, first, last),
        out_shape=out_shape,
        in_specs=[pl.BlockSpec(memory_space=pltpu.SMEM)] + [vmem] * (len(operands) - 1),
        out_specs=vmem if last else (vmem,) * 3,
        scratch_shapes=[pltpu.VMEM((rows, keys, width), queries.dtype)],
        cost_estimate=pl.CostEstimate(
            flops=2 * rows * tall * keys * (width + KV_RANK),
            bytes_accessed=2 * rows * (keys + tall) * width,
            transcendentals=rows * tall * keys,
        ),
        compiler_params=pltpu.CompilerParams(vmem_limit_bytes=ATTEND_VMEM),
        name="attend_last" if last else "attend",
    )(*operands)


def spread_exchange(local, assign, row_place, row_count, rows_here):
    group_rows = local.shape[0]
    most_slots = min(rows_here, max(2, 2 * rows_here * SPR // row_count))
    home_group = row_place // SPR
    dest_prompt = assign.reshape(row_count, rows_here)
    in_group = dest_prompt // group_rows == home_group
    rank = jnp.cumsum(in_group.astype(jnp.int32), axis=1) - 1
    slot_ids = jnp.arange(most_slots, dtype=jnp.int32)
    picked = in_group[:, :, None] & (rank[:, :, None] == slot_ids[None, None, :])
    local_id = dest_prompt - home_group * group_rows
    source_index = jnp.sum(jnp.where(picked, local_id[:, :, None], 0), axis=1)
    rows_taken = jnp.take(local, source_index.reshape(-1), axis=0)
    moved = lax.all_to_all(
        rows_taken.reshape((row_count, most_slots) + local.shape[1:]),
        "row",
        split_axis=0,
        concat_axis=0,
        tiled=True,
    )
    owned = lax.dynamic_slice_in_dim(assign, row_place * rows_here, rows_here)
    owned_group = owned // group_rows
    row_ids = jnp.arange(rows_here, dtype=jnp.int32)
    same_before = (owned_group[:, None] == owned_group[None, :]) & (
        row_ids[None, :] < row_ids[:, None]
    )
    own_rank = jnp.sum(same_before.astype(jnp.int32), axis=1)
    flat = moved.reshape((row_count * most_slots,) + local.shape[1:])
    place = row_place % SPR
    chunks = []
    for offset in range(SPR):
        index = (owned_group * SPR + (place ^ offset)) * most_slots + own_rank
        chunks.append(jnp.take(flat, index, axis=0))
    return chunks


def shards(prompt_latent, row_cache, queries, new_latent, prompt_len, assign, row_ctx):
    row_count = lax.axis_size("row")
    row_place = lax.axis_index("row")
    side = lax.axis_index("tp")
    rows_here = row_cache.shape[0]
    local = prompt_latent[0]
    place = row_place % SPR
    swap = [(0, 1), (1, 0)]
    if row_count == SPR:
        packed = dict(zip(SEND_ORDER, pack(SEND_ORDER, assign, row_place, local, rows_here)))
        mine = {}
        for offset in SEND_ORDER:
            pairs = [(i, i ^ offset) for i in range(row_count)]
            mine[offset] = lax.ppermute(packed[offset], "row", pairs)
        mine[0] = pack((0,), assign, row_place, local, rows_here)[0]
    else:
        mine = dict(enumerate(spread_exchange(local, assign, row_place, row_count, rows_here)))
    theirs = {}
    for stage in STAGES:
        for offset in stage:
            theirs[offset] = lax.ppermute(mine[offset], "tp", swap)
    owned = lax.dynamic_slice_in_dim(assign, row_place * rows_here, rows_here)
    live_len = jnp.take(prompt_len, owned)
    info = jnp.concatenate([live_len, row_ctx, place[None], side[None]]).astype(jnp.int32)
    fresh = jnp.swapaxes(new_latent, 0, 1)
    carry = None
    for number, stage in enumerate(STAGES):
        carry = attend(
            stage,
            info,
            queries,
            [mine[offset] for offset in stage],
            [theirs[offset] for offset in stage],
            row_cache,
            fresh,
            carry,
            number == len(STAGES) - 1,
        )
    return carry


def solution(mesh):
    return jax.shard_map(
        shards,
        mesh=mesh,
        in_specs=(
            P(("group", "row"), None, "tp", None),
            P(("group", "row"), None, None),
            P(None, ("group", "row"), "tp", None),
            P(None, ("group", "row"), None),
            P("group"),
            P("group"),
            P(("group", "row")),
        ),
        out_specs=P(None, ("group", "row"), "tp", None),
        check_vma=False,
    )
```

```python
import functools

import jax
import jax.numpy as jnp
from jax import lax
from jax.experimental import pallas as pl
from jax.experimental.pallas import tpu as pltpu
from jax.sharding import PartitionSpec as P


KV_RANK = 512
ROPE_DIM = 64
NOPE_DIM = 128
SPR = 8

PACK_VMEM = 4 << 20
ATTEND_VMEM = 16 << 20

SEND_ORDER = (4, 5, 2, 3, 1, 6, 7)
STAGES = ((0,), (4, 5), (1, 2, 3), (6,), (7,))


def write_bias(bias_ref, lives, caches, place, side, piece):
    block = 2 * piece
    lane = lax.broadcasted_iota(jnp.int32, (1, block), 1)
    spot = jnp.where(lane < piece, side * piece + lane, (1 - side) * piece + lane - piece)
    rows, cached = len(lives), bias_ref.shape[1] - SPR * block
    slot = lax.broadcasted_iota(jnp.int32, (1, cached), 1)
    for r in range(rows):
        for offset in range(SPR):
            live = spot + (place ^ offset) * block < lives[r]
            bias_ref[r : r + 1, offset * block : (offset + 1) * block] = jnp.where(
                live, 0.0, -jnp.inf
            )
        bias_ref[r : r + 1, SPR * block :] = jnp.where(slot < caches[r], 0.0, -jnp.inf)


def join_rows(rows):
    return jnp.concatenate(
        [row[:, :KV_RANK] for row in rows] + [row[:, KV_RANK:] for row in rows], axis=1
    )


def pack_kernel(order, assign_hbm, length_hbm, ctx_hbm, latent_hbm, *refs):
    outs, bias_ref = refs[: len(order)], refs[len(order)]
    assign_ref, length_ref, ctx_ref, latent_ref, sems, small_sems = refs[len(order) + 1 :]
    rows_here = ctx_hbm.shape[0]
    place, side = lax.axis_index("row"), lax.axis_index("tp")
    smalls = [
        pltpu.make_async_copy(src, dst, small_sems.at[i])
        for i, (src, dst) in enumerate(
            ((assign_hbm, assign_ref), (length_hbm, length_ref), (ctx_hbm, ctx_ref))
        )
    ]
    copies = [
        pltpu.make_async_copy(latent_hbm.at[p], latent_ref.at[p], sems.at[p])
        for p in range(latent_hbm.shape[0])
    ]
    for copy in smalls + copies:
        copy.start()
    for copy in smalls:
        copy.wait()
    lives = [length_ref[assign_ref[place * rows_here + r]] for r in range(rows_here)]
    caches = [ctx_ref[r] for r in range(rows_here)]
    write_bias(bias_ref, lives, caches, place, side, latent_hbm.shape[1])
    for copy in copies:
        copy.wait()
    for out, offset in zip(outs, order):
        first = (place ^ offset) * rows_here
        out[...] = join_rows([latent_ref[assign_ref[first + r]] for r in range(rows_here)])


def pack(order, assign, prompt_len, row_ctx, local, cached):
    rows_here = row_ctx.shape[0]
    piece, width = local.shape[1:]
    hbm = pl.BlockSpec(memory_space=pltpu.HBM)
    vmem = pl.BlockSpec(memory_space=pltpu.VMEM)
    operands = [
        pltpu.with_memory_space_constraint(x, pltpu.HBM)
        for x in (assign, prompt_len, row_ctx, local)
    ]
    out = pl.pallas_call(
        functools.partial(pack_kernel, order),
        out_shape=[jax.ShapeDtypeStruct((piece, rows_here * width), local.dtype) for _ in order]
        + [jax.ShapeDtypeStruct((rows_here, SPR * 2 * piece + cached), jnp.float32)],
        in_specs=[hbm] * 4,
        out_specs=[vmem] * (len(order) + 1),
        scratch_shapes=[
            pltpu.SMEM(assign.shape, jnp.int32),
            pltpu.SMEM(prompt_len.shape, jnp.int32),
            pltpu.SMEM(row_ctx.shape, jnp.int32),
            pltpu.VMEM(local.shape, local.dtype),
            pltpu.SemaphoreType.DMA((local.shape[0],)),
            pltpu.SemaphoreType.DMA((3,)),
        ],
        compiler_params=pltpu.CompilerParams(vmem_limit_bytes=PACK_VMEM),
        name="pack",
    )(*operands)
    return dict(zip(order, out)), out[-1]


def spread_kernel(q_ref, out_ref):
    steps, rows, heads, width = q_ref.shape
    rope = width - KV_RANK
    for r in range(rows):
        query = q_ref[:, r].reshape(steps * heads, width)
        out_ref[r, :, :KV_RANK] = query[:, :KV_RANK]
        blank = jnp.zeros((steps * heads, rope), query.dtype)
        tail = [query[:, KV_RANK:] if other == r else blank for other in range(rows)]
        out_ref[r, :, KV_RANK:] = jnp.concatenate(tail, axis=1)


def spread_queries(queries):
    steps, rows, heads, width = queries.shape
    wide = KV_RANK + rows * (width - KV_RANK)
    vmem = pl.BlockSpec(memory_space=pltpu.VMEM)
    return pl.pallas_call(
        spread_kernel,
        out_shape=jax.ShapeDtypeStruct((rows, steps * heads, wide), queries.dtype),
        in_specs=[vmem],
        out_specs=vmem,
        compiler_params=pltpu.CompilerParams(vmem_limit_bytes=PACK_VMEM),
        name="spread",
    )(queries)


def attend_kernel(offsets, heads, first, last, bias_ref, q_ref, *refs):
    refs = list(refs)
    own = [refs.pop(0) for _ in offsets]
    other = [refs.pop(0) for _ in offsets]
    if first:
        cache_ref, new_ref = refs.pop(0), refs.pop(0)
    else:
        top_in, sum_in, acc_in = refs.pop(0), refs.pop(0), refs.pop(0)
    if last:
        out_ref = refs.pop(0)
    else:
        top_out, sum_out, acc_out = refs.pop(0), refs.pop(0), refs.pop(0)
    keys_ref = refs.pop(0)
    rows, tall, _ = q_ref.shape
    piece = own[0].shape[0]
    block = 2 * piece
    scale = (NOPE_DIM + ROPE_DIM) ** -0.5
    by_width = (((1,), (1,)), ((), ()))
    dot = functools.partial(lax.dot_general, preferred_element_type=jnp.float32)
    for r in range(rows):
        biases = []
        for i, offset in enumerate(offsets):
            for half, start in ((own[i], i * block), (other[i], i * block + piece)):
                spot = slice(start, start + piece)
                keys_ref[r, spot, :KV_RANK] = half[:, r * KV_RANK : (r + 1) * KV_RANK]
                keys_ref[r, spot, KV_RANK:] = half[:, rows * KV_RANK :]
            biases.append(bias_ref[r : r + 1, offset * block : (offset + 1) * block])
        query = q_ref[r]
        scores = [dot(query, keys_ref[r], by_width) * scale + jnp.concatenate(biases, axis=1)]
        values = [lambda w, r=r: jnp.dot(w, keys_ref[r, :, :KV_RANK], preferred_element_type=jnp.float32)]
        if first:
            rope = new_ref.shape[2] - KV_RANK
            rotary = query[:, KV_RANK + r * rope : KV_RANK + (r + 1) * rope]
            narrow = jnp.concatenate([query[:, :KV_RANK], rotary], axis=1)
            cached = dot(narrow, cache_ref[r], (((1,), (0,)), ((), ())))
            scores.append(cached * scale + bias_ref[r : r + 1, SPR * block :])
            values.append(lambda w, r=r: dot(w, cache_ref[r, :KV_RANK], by_width))
            fresh = dot(narrow, new_ref[r], by_width)
            step = lax.broadcasted_iota(jnp.int32, fresh.shape, 0) // heads
            slot = lax.broadcasted_iota(jnp.int32, fresh.shape, 1)
            scores.append(jnp.where(slot <= step, fresh * scale, -jnp.inf))
            values.append(
                lambda w, r=r: jnp.dot(w, new_ref[r, :, :KV_RANK], preferred_element_type=jnp.float32)
            )
        tops = [jnp.max(part, axis=1, keepdims=True) for part in scores]
        if not first:
            tops.append(top_in[r])
        top = functools.reduce(jnp.maximum, tops)
        weights = [jnp.exp(part - top) for part in scores]
        total = sum(jnp.sum(weight, axis=1, keepdims=True) for weight in weights)
        acc = sum(value(weight.astype(q_ref.dtype)) for weight, value in zip(weights, values))
        if not first:
            shrink = jnp.exp(top_in[r] - top)
            total += shrink * sum_in[r]
            acc += shrink * acc_in[r]
        if last:
            out = (acc / total).astype(out_ref.dtype)
            out_ref[:, r] = out.reshape(tall // heads, heads, KV_RANK)
        else:
            top_out[r] = top
            sum_out[r] = total
            acc_out[r] = acc


def attend(offsets, bias, wide, own, other, shape, cache=None, fresh=None, carry=None, last=False):
    rows, tall, width = wide.shape
    heads = shape[2]
    first = carry is None
    keys = 2 * own[0].shape[0] * len(offsets)
    state = (
        jax.ShapeDtypeStruct((rows, tall, 1), jnp.float32),
        jax.ShapeDtypeStruct((rows, tall, 1), jnp.float32),
        jax.ShapeDtypeStruct((rows, tall, KV_RANK), jnp.float32),
    )
    out_shape = jax.ShapeDtypeStruct(shape[:3] + (KV_RANK,), wide.dtype) if last else state
    extra = (cache, fresh) if first else carry
    operands = (bias, wide, *own, *other, *extra)
    vmem = pl.BlockSpec(memory_space=pltpu.VMEM)
    return pl.pallas_call(
        functools.partial(attend_kernel, offsets, heads, first, last),
        out_shape=out_shape,
        in_specs=[vmem] * len(operands),
        out_specs=vmem if last else (vmem,) * 3,
        scratch_shapes=[pltpu.VMEM((rows, keys, width), wide.dtype)],
        cost_estimate=pl.CostEstimate(
            flops=2 * rows * tall * keys * (width + KV_RANK),
            bytes_accessed=2 * rows * (keys + tall) * width,
            transcendentals=rows * tall * keys,
        ),
        compiler_params=pltpu.CompilerParams(vmem_limit_bytes=ATTEND_VMEM),
        name="attend_last" if last else "attend",
    )(*operands)


def spread_exchange(local, assign, row_place, row_count, rows_here):
    group_rows = local.shape[0]
    most_slots = min(rows_here, max(2, 2 * rows_here * SPR // row_count))
    home_group = row_place // SPR
    dest_prompt = assign.reshape(row_count, rows_here)
    in_group = dest_prompt // group_rows == home_group
    rank = jnp.cumsum(in_group.astype(jnp.int32), axis=1) - 1
    slot_ids = jnp.arange(most_slots, dtype=jnp.int32)
    picked = in_group[:, :, None] & (rank[:, :, None] == slot_ids[None, None, :])
    local_id = dest_prompt - home_group * group_rows
    source_index = jnp.sum(jnp.where(picked, local_id[:, :, None], 0), axis=1)
    rows_taken = jnp.take(local, source_index.reshape(-1), axis=0)
    moved = lax.all_to_all(
        rows_taken.reshape((row_count, most_slots) + local.shape[1:]),
        "row",
        split_axis=0,
        concat_axis=0,
        tiled=True,
    )
    owned = lax.dynamic_slice_in_dim(assign, row_place * rows_here, rows_here)
    owned_group = owned // group_rows
    row_ids = jnp.arange(rows_here, dtype=jnp.int32)
    same_before = (owned_group[:, None] == owned_group[None, :]) & (
        row_ids[None, :] < row_ids[:, None]
    )
    own_rank = jnp.sum(same_before.astype(jnp.int32), axis=1)
    flat = moved.reshape((row_count * most_slots,) + local.shape[1:])
    place = row_place % SPR
    chunks = {}
    for offset in range(SPR):
        index = (owned_group * SPR + (place ^ offset)) * most_slots + own_rank
        taken = jnp.take(flat, index, axis=0)
        chunks[offset] = join_rows([taken[r] for r in range(rows_here)])
    return chunks


def spread_bias(assign, prompt_len, row_ctx, row_place, side, piece, cached):
    rows_here = row_ctx.shape[0]
    owned = lax.dynamic_slice_in_dim(assign, row_place * rows_here, rows_here)
    lives = jnp.take(prompt_len, owned)
    lane = jnp.arange(2 * piece, dtype=jnp.int32)
    spot = jnp.where(lane < piece, side * piece + lane, (1 - side) * piece + lane - piece)
    block = (row_place % SPR) ^ jnp.arange(SPR, dtype=jnp.int32)
    spots = (spot[None, :] + block[:, None] * 2 * piece).reshape(1, -1)
    slots = jnp.arange(cached, dtype=jnp.int32)[None, :]
    live = jnp.concatenate([spots < lives[:, None], slots < row_ctx[:, None]], axis=1)
    return jnp.where(live, 0.0, -jnp.inf).astype(jnp.float32)


def shards(prompt_latent, row_cache, queries, new_latent, prompt_len, assign, row_ctx):
    row_count = lax.axis_size("row")
    rows_here, cached = row_cache.shape[:2]
    local = prompt_latent[0]
    if row_count == SPR:
        packed, bias = pack((0,) + SEND_ORDER, assign, prompt_len, row_ctx, local, cached)
        mine = {0: packed[0]}
        for offset in SEND_ORDER:
            pairs = [(i, i ^ offset) for i in range(row_count)]
            mine[offset] = lax.ppermute(packed[offset], "row", pairs)
    else:
        row_place, side = lax.axis_index("row"), lax.axis_index("tp")
        mine = spread_exchange(local, assign, row_place, row_count, rows_here)
        bias = spread_bias(assign, prompt_len, row_ctx, row_place, side, local.shape[1], cached)
    theirs = {}
    for stage in STAGES:
        for offset in stage:
            theirs[offset] = lax.ppermute(mine[offset], "tp", [(0, 1), (1, 0)])
    fresh = jnp.swapaxes(new_latent, 0, 1)
    wide = spread_queries(queries)
    carry = None
    for number, stage in enumerate(STAGES):
        carry = attend(
            stage,
            bias,
            wide,
            [mine[offset] for offset in stage],
            [theirs[offset] for offset in stage],
            queries.shape,
            jnp.swapaxes(row_cache, 1, 2),
            fresh,
            carry,
            number == len(STAGES) - 1,
        )
    return carry


def solution(mesh):
    return jax.shard_map(
        shards,
        mesh=mesh,
        in_specs=(
            P(("group", "row"), None, "tp", None),
            P(("group", "row"), None, None),
            P(None, ("group", "row"), "tp", None),
            P(None, ("group", "row"), None),
            P("group"),
            P("group"),
            P(("group", "row")),
        ),
        out_specs=P(None, ("group", "row"), "tp", None),
        check_vma=False,
    )
```

```python
import functools

import jax
import jax.numpy as jnp
from jax import lax
from jax.experimental import pallas as pl
from jax.experimental.pallas import tpu as pltpu
from jax.sharding import PartitionSpec as P


KV_RANK = 512
ROPE_DIM = 64
NOPE_DIM = 128
SPR = 8

PACK_VMEM = 4 << 20
ATTEND_VMEM = 16 << 20

SEND_ORDER = (4, 5, 2, 3, 1, 6, 7)
STAGES = ((0,), (4, 5), (1, 2, 3, 6), (7,))


def write_bias(bias_ref, lives, caches, place, side, piece):
    block = 2 * piece
    lane = lax.broadcasted_iota(jnp.int32, (1, block), 1)
    spot = jnp.where(lane < piece, side * piece + lane, (1 - side) * piece + lane - piece)
    rows, cached = len(lives), bias_ref.shape[1] - SPR * block
    slot = lax.broadcasted_iota(jnp.int32, (1, cached), 1)
    for r in range(rows):
        for offset in range(SPR):
            live = spot + (place ^ offset) * block < lives[r]
            bias_ref[r : r + 1, offset * block : (offset + 1) * block] = jnp.where(
                live, 0.0, -jnp.inf
            )
        bias_ref[r : r + 1, SPR * block :] = jnp.where(slot < caches[r], 0.0, -jnp.inf)


def join_rows(rows):
    return jnp.concatenate(
        [row[:, :KV_RANK] for row in rows] + [row[:, KV_RANK:] for row in rows], axis=1
    )


def pack_kernel(order, assign_hbm, length_hbm, ctx_hbm, latent_hbm, *refs):
    outs, bias_ref = refs[: len(order)], refs[len(order)]
    assign_ref, length_ref, ctx_ref, latent_ref, sems, small_sems = refs[len(order) + 1 :]
    rows_here = ctx_hbm.shape[0]
    place, side = lax.axis_index("row"), lax.axis_index("tp")
    smalls = [
        pltpu.make_async_copy(src, dst, small_sems.at[i])
        for i, (src, dst) in enumerate(
            ((assign_hbm, assign_ref), (length_hbm, length_ref), (ctx_hbm, ctx_ref))
        )
    ]
    copies = [
        pltpu.make_async_copy(latent_hbm.at[p], latent_ref.at[p], sems.at[p])
        for p in range(latent_hbm.shape[0])
    ]
    for copy in smalls + copies:
        copy.start()
    for copy in smalls:
        copy.wait()
    lives = [length_ref[assign_ref[place * rows_here + r]] for r in range(rows_here)]
    caches = [ctx_ref[r] for r in range(rows_here)]
    write_bias(bias_ref, lives, caches, place, side, latent_hbm.shape[1])
    for copy in copies:
        copy.wait()
    for out, offset in zip(outs, order):
        first = (place ^ offset) * rows_here
        out[...] = join_rows([latent_ref[assign_ref[first + r]] for r in range(rows_here)])


def in_hbm(*arrays):
    return [pltpu.with_memory_space_constraint(x, pltpu.HBM) for x in arrays]


def pack(order, assign, prompt_len, row_ctx, local, cached):
    rows_here = row_ctx.shape[0]
    count, piece, width = local.shape
    hbm, vmem = pl.BlockSpec(memory_space=pltpu.HBM), pl.BlockSpec(memory_space=pltpu.VMEM)
    out = pl.pallas_call(
        functools.partial(pack_kernel, order),
        out_shape=[jax.ShapeDtypeStruct((piece, rows_here * width), local.dtype) for _ in order]
        + [jax.ShapeDtypeStruct((rows_here, SPR * 2 * piece + cached), jnp.float32)],
        in_specs=[hbm] * 4,
        out_specs=[vmem] * (len(order) + 1),
        scratch_shapes=[
            pltpu.SMEM(assign.shape, jnp.int32),
            pltpu.SMEM(prompt_len.shape, jnp.int32),
            pltpu.SMEM(row_ctx.shape, jnp.int32),
            pltpu.VMEM(local.shape, local.dtype),
            pltpu.SemaphoreType.DMA((count,)),
            pltpu.SemaphoreType.DMA((3,)),
        ],
        compiler_params=pltpu.CompilerParams(vmem_limit_bytes=PACK_VMEM),
        name="pack",
    )(*in_hbm(assign, prompt_len, row_ctx, local))
    return dict(zip(order, out)), out[-1]


def spread_kernel(q_hbm, cache_hbm, out_ref, cache_ref, q_ref, sems):
    copies = [
        pltpu.make_async_copy(q_hbm, q_ref, sems.at[0]),
        pltpu.make_async_copy(cache_hbm, cache_ref, sems.at[1]),
    ]
    for copy in copies:
        copy.start()
    copies[0].wait()
    steps, rows, heads, width = q_ref.shape
    rope = width - KV_RANK
    for r in range(rows):
        query = q_ref[:, r].reshape(steps * heads, width)
        out_ref[r, :, :KV_RANK] = query[:, :KV_RANK]
        blank = jnp.zeros((steps * heads, rope), query.dtype)
        tail = [query[:, KV_RANK:] if other == r else blank for other in range(rows)]
        out_ref[r, :, KV_RANK:] = jnp.concatenate(tail, axis=1)
    copies[1].wait()


def spread_queries(queries, turned):
    steps, rows, heads, width = queries.shape
    wide = KV_RANK + rows * (width - KV_RANK)
    hbm, vmem = pl.BlockSpec(memory_space=pltpu.HBM), pl.BlockSpec(memory_space=pltpu.VMEM)
    return pl.pallas_call(
        spread_kernel,
        out_shape=[
            jax.ShapeDtypeStruct((rows, steps * heads, wide), queries.dtype),
            jax.ShapeDtypeStruct(turned.shape, turned.dtype),
        ],
        in_specs=[hbm] * 2,
        out_specs=[vmem] * 2,
        scratch_shapes=[
            pltpu.VMEM(queries.shape, queries.dtype),
            pltpu.SemaphoreType.DMA((2,)),
        ],
        compiler_params=pltpu.CompilerParams(vmem_limit_bytes=PACK_VMEM),
        name="spread",
    )(*in_hbm(queries, turned))


def attend_kernel(offsets, heads, first, last, bias_ref, q_ref, *refs):
    refs = list(refs)
    own = [refs.pop(0) for _ in offsets]
    other = [refs.pop(0) for _ in offsets]
    if first:
        cache_ref, new_ref = refs.pop(0), refs.pop(0)
    else:
        top_in, sum_in, acc_in = refs.pop(0), refs.pop(0), refs.pop(0)
    if last:
        out_ref, stage_ref, sems = refs
    else:
        top_out, sum_out, acc_out = refs
    rows, tall, _ = q_ref.shape
    piece = own[0].shape[0]
    block = 2 * piece
    scale = (NOPE_DIM + ROPE_DIM) ** -0.5
    by_width = (((1,), (1,)), ((), ()))
    dot = functools.partial(lax.dot_general, preferred_element_type=jnp.float32)
    for r in range(rows):
        halves = [half for pair in zip(own, other) for half in pair]
        value = jnp.concatenate([h[:, r * KV_RANK : (r + 1) * KV_RANK] for h in halves], axis=0)
        rotary = jnp.concatenate([h[:, rows * KV_RANK :] for h in halves], axis=0)
        biases = [bias_ref[r : r + 1, i * block : (i + 1) * block] for i in offsets]
        query = q_ref[r]
        found = dot(query, jnp.concatenate([value, rotary], axis=1), by_width)
        scores = [found * scale + jnp.concatenate(biases, axis=1)]
        values = [lambda w, v=value: jnp.dot(w, v, preferred_element_type=jnp.float32)]
        if first:
            rope = new_ref.shape[2] - KV_RANK
            turn = query[:, KV_RANK + r * rope : KV_RANK + (r + 1) * rope]
            narrow = jnp.concatenate([query[:, :KV_RANK], turn], axis=1)
            cached = dot(narrow, cache_ref[r], (((1,), (0,)), ((), ())))
            scores.append(cached * scale + bias_ref[r : r + 1, SPR * block :])
            values.append(lambda w, r=r: dot(w, cache_ref[r, :KV_RANK], by_width))
            fresh = dot(narrow, new_ref[r], by_width)
            step = lax.broadcasted_iota(jnp.int32, fresh.shape, 0) // heads
            slot = lax.broadcasted_iota(jnp.int32, fresh.shape, 1)
            scores.append(jnp.where(slot <= step, fresh * scale, -jnp.inf))
            values.append(
                lambda w, r=r: jnp.dot(w, new_ref[r, :, :KV_RANK], preferred_element_type=jnp.float32)
            )
        tops = [jnp.max(part, axis=1, keepdims=True) for part in scores]
        if not first:
            tops.append(top_in[r])
        top = functools.reduce(jnp.maximum, tops)
        weights = [jnp.exp(part - top) for part in scores]
        total = sum(jnp.sum(weight, axis=1, keepdims=True) for weight in weights)
        acc = sum(times(weight.astype(q_ref.dtype)) for weight, times in zip(weights, values))
        if not first:
            shrink = jnp.exp(top_in[r] - top)
            total += shrink * sum_in[r]
            acc += shrink * acc_in[r]
        if last:
            out = (acc * (1.0 / total)).astype(out_ref.dtype)
            stage_ref[r] = out.reshape(tall // heads, heads, KV_RANK)
            copies = [
                pltpu.make_async_copy(stage_ref.at[r, s], out_ref.at[s, r], sems.at[r, s])
                for s in range(tall // heads)
            ]
            for copy in copies:
                copy.start()
        else:
            top_out[r] = top
            sum_out[r] = total
            acc_out[r] = acc
    if last:
        for r in range(rows):
            for s in range(tall // heads):
                pltpu.make_async_copy(stage_ref.at[r, s], out_ref.at[s, r], sems.at[r, s]).wait()


def attend(offsets, bias, wide, own, other, shape, cache, fresh, carry, last):
    rows, tall, width = wide.shape
    steps, heads = shape[0], shape[2]
    first = carry is None
    keys = 2 * own[0].shape[0] * len(offsets)
    state = (
        jax.ShapeDtypeStruct((rows, tall, 1), jnp.float32),
        jax.ShapeDtypeStruct((rows, tall, 1), jnp.float32),
        jax.ShapeDtypeStruct((rows, tall, KV_RANK), jnp.float32),
    )
    final = (steps, rows, heads, KV_RANK)
    operands = (bias, wide, *own, *other, *((cache, fresh) if first else carry))
    vmem, hbm = pl.BlockSpec(memory_space=pltpu.VMEM), pl.BlockSpec(memory_space=pltpu.HBM)
    scratch = []
    if last:
        scratch = [
            pltpu.VMEM((rows, steps, heads, KV_RANK), wide.dtype),
            pltpu.SemaphoreType.DMA((rows, steps)),
        ]
    return pl.pallas_call(
        functools.partial(attend_kernel, offsets, heads, first, last),
        out_shape=jax.ShapeDtypeStruct(final, wide.dtype) if last else state,
        in_specs=[vmem] * len(operands),
        out_specs=hbm if last else (vmem,) * 3,
        scratch_shapes=scratch,
        cost_estimate=pl.CostEstimate(
            flops=2 * rows * tall * keys * (width + KV_RANK),
            bytes_accessed=2 * rows * (keys + tall) * width,
            transcendentals=rows * tall * keys,
        ),
        compiler_params=pltpu.CompilerParams(vmem_limit_bytes=ATTEND_VMEM),
        name="attend_last" if last else "attend",
    )(*operands)


def spread_exchange(local, assign, row_place, row_count, rows_here):
    group_rows = local.shape[0]
    most_slots = min(rows_here, max(2, 2 * rows_here * SPR // row_count))
    home_group = row_place // SPR
    dest_prompt = assign.reshape(row_count, rows_here)
    in_group = dest_prompt // group_rows == home_group
    rank = jnp.cumsum(in_group.astype(jnp.int32), axis=1) - 1
    slot_ids = jnp.arange(most_slots, dtype=jnp.int32)
    picked = in_group[:, :, None] & (rank[:, :, None] == slot_ids[None, None, :])
    local_id = dest_prompt - home_group * group_rows
    source_index = jnp.sum(jnp.where(picked, local_id[:, :, None], 0), axis=1)
    rows_taken = jnp.take(local, source_index.reshape(-1), axis=0)
    moved = lax.all_to_all(
        rows_taken.reshape((row_count, most_slots) + local.shape[1:]),
        "row",
        split_axis=0,
        concat_axis=0,
        tiled=True,
    )
    owned = lax.dynamic_slice_in_dim(assign, row_place * rows_here, rows_here)
    owned_group = owned // group_rows
    row_ids = jnp.arange(rows_here, dtype=jnp.int32)
    same_before = (owned_group[:, None] == owned_group[None, :]) & (
        row_ids[None, :] < row_ids[:, None]
    )
    own_rank = jnp.sum(same_before.astype(jnp.int32), axis=1)
    flat = moved.reshape((row_count * most_slots,) + local.shape[1:])
    place = row_place % SPR
    chunks = {}
    for offset in range(SPR):
        index = (owned_group * SPR + (place ^ offset)) * most_slots + own_rank
        taken = jnp.take(flat, index, axis=0)
        chunks[offset] = join_rows([taken[r] for r in range(rows_here)])
    return chunks


def spread_bias(assign, prompt_len, row_ctx, row_place, side, piece, cached):
    rows_here = row_ctx.shape[0]
    owned = lax.dynamic_slice_in_dim(assign, row_place * rows_here, rows_here)
    lives = jnp.take(prompt_len, owned)
    lane = jnp.arange(2 * piece, dtype=jnp.int32)
    spot = jnp.where(lane < piece, side * piece + lane, (1 - side) * piece + lane - piece)
    block = (row_place % SPR) ^ jnp.arange(SPR, dtype=jnp.int32)
    spots = (spot[None, :] + block[:, None] * 2 * piece).reshape(1, -1)
    slots = jnp.arange(cached, dtype=jnp.int32)[None, :]
    live = jnp.concatenate([spots < lives[:, None], slots < row_ctx[:, None]], axis=1)
    return jnp.where(live, 0.0, -jnp.inf).astype(jnp.float32)


def shards(prompt_latent, row_cache, queries, new_latent, prompt_len, assign, row_ctx):
    row_count = lax.axis_size("row")
    rows_here, cached = row_cache.shape[:2]
    local = prompt_latent[0]
    if row_count == SPR:
        packed, bias = pack(SEND_ORDER + (0,), assign, prompt_len, row_ctx, local, cached)
        mine = {0: packed[0]}
        for offset in SEND_ORDER:
            pairs = [(i, i ^ offset) for i in range(row_count)]
            mine[offset] = lax.ppermute(packed[offset], "row", pairs)
    else:
        row_place, side = lax.axis_index("row"), lax.axis_index("tp")
        mine = spread_exchange(local, assign, row_place, row_count, rows_here)
        bias = spread_bias(assign, prompt_len, row_ctx, row_place, side, local.shape[1], cached)
    theirs = {}
    for stage in STAGES:
        for offset in stage:
            theirs[offset] = lax.ppermute(mine[offset], "tp", [(0, 1), (1, 0)])
    fresh = jnp.swapaxes(new_latent, 0, 1)
    wide, turned = spread_queries(queries, jnp.swapaxes(row_cache, 1, 2))
    carry = None
    for number, stage in enumerate(STAGES):
        own, other = [mine[offset] for offset in stage], [theirs[offset] for offset in stage]
        last = number == len(STAGES) - 1
        carry = attend(
            stage, bias, wide, own, other, queries.shape, turned, fresh, carry, last
        )
    return carry


def solution(mesh):
    return jax.shard_map(
        shards,
        mesh=mesh,
        in_specs=(
            P(("group", "row"), None, "tp", None),
            P(("group", "row"), None, None),
            P(None, ("group", "row"), "tp", None),
            P(None, ("group", "row"), None),
            P("group"),
            P("group"),
            P(("group", "row")),
        ),
        out_specs=P(None, ("group", "row"), "tp", None),
        check_vma=False,
    )
```

```python
import functools

import jax
import jax.numpy as jnp
from jax import lax
from jax.experimental import pallas as pl
from jax.experimental.pallas import tpu as pltpu
from jax.sharding import PartitionSpec as P


KV_RANK = 512
ROPE_DIM = 64
NOPE_DIM = 128
SPR = 8
LANES = 128

PACK_VMEM = 4 << 20
ATTEND_VMEM = 16 << 20

SEND_ORDER = (4, 5, 2, 3, 11, 10, 6)
STAGES = ((0,), (4, 5), (2, 3, 11), (10, 6))
ROUNDS = sum(STAGES, ())
MIXED = {10: (7, 1), 11: (1, 7)}


def partner(number, place):
    if number not in MIXED:
        return place ^ number
    inner, outer = MIXED[number]
    middle = ((place >> 1) ^ (place >> 2)) & 1
    return place ^ (middle * inner + (1 - middle) * outer)


def write_bias(bias_ref, lives, caches, place, side, piece):
    block = 2 * piece
    rows, keys, lanes = bias_ref.shape
    slot = lax.broadcasted_iota(jnp.int32, (block, lanes), 0)
    spot = jnp.where(slot < piece, side * piece + slot, (1 - side) * piece + slot - piece)
    kept = lax.broadcasted_iota(jnp.int32, (keys - SPR * block, lanes), 0)
    for r in range(rows):
        for i, number in enumerate(ROUNDS):
            live = spot + partner(number, place) * block < lives[r]
            bias_ref[r, i * block : (i + 1) * block] = jnp.where(live, 0.0, -jnp.inf)
        bias_ref[r, SPR * block :] = jnp.where(kept < caches[r], 0.0, -jnp.inf)


def join_rows(rows):
    return jnp.concatenate(
        [row[:, :KV_RANK] for row in rows] + [row[:, KV_RANK:] for row in rows], axis=1
    )


def pack_kernel(order, rows_here, assign_hbm, latent_hbm, *refs):
    outs, (assign_ref, latent_ref, sems) = refs[: len(order)], refs[len(order) :]
    copies = [
        pltpu.make_async_copy(assign_hbm, assign_ref, sems.at[0]),
        pltpu.make_async_copy(latent_hbm, latent_ref, sems.at[1]),
    ]
    for copy in copies:
        copy.start()
    for copy in copies:
        copy.wait()
    place = lax.axis_index("row")
    for out, offset in zip(outs, order):
        first = partner(offset, place) * rows_here
        out[...] = join_rows([latent_ref[assign_ref[first + r]] for r in range(rows_here)])


def in_hbm(*arrays):
    return [pltpu.with_memory_space_constraint(x, pltpu.HBM) for x in arrays]


def pack(order, assign, local, rows_here):
    _, piece, width = local.shape
    vmem = pl.BlockSpec(memory_space=pltpu.VMEM)
    out = pl.pallas_call(
        functools.partial(pack_kernel, order, rows_here),
        out_shape=[jax.ShapeDtypeStruct((piece, rows_here * width), local.dtype) for _ in order],
        in_specs=[pl.BlockSpec(memory_space=pltpu.HBM)] * 2,
        out_specs=[vmem] * len(order),
        scratch_shapes=[
            pltpu.SMEM(assign.shape, jnp.int32),
            pltpu.VMEM(local.shape, local.dtype),
            pltpu.SemaphoreType.DMA((2,)),
        ],
        compiler_params=pltpu.CompilerParams(vmem_limit_bytes=PACK_VMEM),
        name="pack",
    )(*in_hbm(assign, local))
    return dict(zip(order, out))


def bias_kernel(piece, assign_hbm, length_hbm, ctx_hbm, bias_ref, assign_ref, length_ref, ctx_ref, sems):
    copies = [
        pltpu.make_async_copy(src, dst, sems.at[i])
        for i, (src, dst) in enumerate(
            ((assign_hbm, assign_ref), (length_hbm, length_ref), (ctx_hbm, ctx_ref))
        )
    ]
    for copy in copies:
        copy.start()
    for copy in copies:
        copy.wait()
    rows_here = ctx_hbm.shape[0]
    place, side = lax.axis_index("row"), lax.axis_index("tp")
    lives = [length_ref[assign_ref[place * rows_here + r]] for r in range(rows_here)]
    caches = [ctx_ref[r] for r in range(rows_here)]
    write_bias(bias_ref, lives, caches, place, side, piece)


def make_bias(assign, prompt_len, row_ctx, piece, cached):
    shape = (row_ctx.shape[0], SPR * 2 * piece + cached, LANES)
    return pl.pallas_call(
        functools.partial(bias_kernel, piece),
        out_shape=jax.ShapeDtypeStruct(shape, jnp.float32),
        in_specs=[pl.BlockSpec(memory_space=pltpu.HBM)] * 3,
        out_specs=pl.BlockSpec(memory_space=pltpu.VMEM),
        scratch_shapes=[
            pltpu.SMEM(assign.shape, jnp.int32),
            pltpu.SMEM(prompt_len.shape, jnp.int32),
            pltpu.SMEM(row_ctx.shape, jnp.int32),
            pltpu.SemaphoreType.DMA((3,)),
        ],
        compiler_params=pltpu.CompilerParams(vmem_limit_bytes=PACK_VMEM),
        name="bias",
    )(*in_hbm(assign, prompt_len, row_ctx))


def spread_kernel(q_hbm, cache_hbm, out_ref, cache_ref, q_ref, sems):
    copies = [
        pltpu.make_async_copy(q_hbm, q_ref, sems.at[0]),
        pltpu.make_async_copy(cache_hbm, cache_ref, sems.at[1]),
    ]
    for copy in copies:
        copy.start()
    copies[0].wait()
    steps, rows, heads, width = q_ref.shape
    rope = width - KV_RANK
    for r in range(rows):
        query = q_ref[:, r].reshape(steps * heads, width)
        out_ref[r, :, :KV_RANK] = query[:, :KV_RANK]
        blank = jnp.zeros((steps * heads, rope), query.dtype)
        tail = [query[:, KV_RANK:] if other == r else blank for other in range(rows)]
        out_ref[r, :, KV_RANK:] = jnp.concatenate(tail, axis=1)
    copies[1].wait()


def spread_queries(queries, turned):
    steps, rows, heads, width = queries.shape
    wide = KV_RANK + rows * (width - KV_RANK)
    hbm, vmem = pl.BlockSpec(memory_space=pltpu.HBM), pl.BlockSpec(memory_space=pltpu.VMEM)
    return pl.pallas_call(
        spread_kernel,
        out_shape=[
            jax.ShapeDtypeStruct((rows, steps * heads, wide), queries.dtype),
            jax.ShapeDtypeStruct(turned.shape, turned.dtype),
        ],
        in_specs=[hbm] * 2,
        out_specs=[vmem] * 2,
        scratch_shapes=[
            pltpu.VMEM(queries.shape, queries.dtype),
            pltpu.SemaphoreType.DMA((2,)),
        ],
        compiler_params=pltpu.CompilerParams(vmem_limit_bytes=PACK_VMEM),
        name="spread",
    )(*in_hbm(queries, turned))


def attend_kernel(offsets, heads, first, last, bias_ref, q_ref, *refs):
    refs = list(refs)
    own = [refs.pop(0) for _ in offsets]
    other = [refs.pop(0) for _ in offsets]
    if first:
        cache_ref, new_ref = refs.pop(0), refs.pop(0)
    else:
        top_in, sum_in, acc_in = refs.pop(0), refs.pop(0), refs.pop(0)
    if last:
        out_ref, stage_ref, sems = refs
    else:
        top_out, sum_out, acc_out = refs
    rows, tall, _ = q_ref.shape
    piece = own[0].shape[0]
    block = 2 * piece
    scale = (NOPE_DIM + ROPE_DIM) ** -0.5
    by_width = (((1,), (1,)), ((), ()))
    by_key = (((0,), (0,)), ((), ()))
    dot = functools.partial(lax.dot_general, preferred_element_type=jnp.float32)

    def mask(r, start, count):
        return jnp.concatenate([bias_ref[r, start : start + count]] * (tall // LANES), axis=1)

    def column(line):
        turned = jnp.broadcast_to(line, (LANES, tall)).T
        return jnp.concatenate([turned] * (KV_RANK // LANES), axis=1)

    every = range(rows)
    halves = [half for pair in zip(own, other) for half in pair]
    value = [
        jnp.concatenate([h[:, r * KV_RANK : (r + 1) * KV_RANK] for h in halves], axis=0)
        for r in every
    ]
    rotary = jnp.concatenate([h[:, rows * KV_RANK :] for h in halves], axis=0)
    scores = []
    for r in every:
        found = dot(jnp.concatenate([value[r], rotary], axis=1), q_ref[r], by_width)
        biases = [mask(r, ROUNDS.index(number) * block, block) for number in offsets]
        scores.append([found * scale + jnp.concatenate(biases, axis=0)])
        if first:
            rope = new_ref.shape[2] - KV_RANK
            turn = q_ref[r, :, KV_RANK + r * rope : KV_RANK + (r + 1) * rope]
            narrow = jnp.concatenate([q_ref[r, :, :KV_RANK], turn], axis=1)
            cached = dot(cache_ref[r], narrow, (((0,), (1,)), ((), ())))
            scores[r].append(cached * scale + mask(r, SPR * block, cached.shape[0]))
            fresh = dot(new_ref[r], narrow, by_width)
            step = lax.broadcasted_iota(jnp.int32, fresh.shape, 1) // heads
            slot = lax.broadcasted_iota(jnp.int32, fresh.shape, 0)
            scores[r].append(jnp.where(slot <= step, fresh * scale, -jnp.inf))
    weights, shrinks = [], []
    for r in every:
        tops = [jnp.max(part, axis=0, keepdims=True) for part in scores[r]]
        if not first:
            tops.append(top_in[r])
        top = functools.reduce(jnp.maximum, tops)
        parts = [jnp.exp(part - top) for part in scores[r]]
        total = sum(jnp.sum(part, axis=0, keepdims=True) for part in parts)
        if not first:
            shrinks.append(jnp.exp(top_in[r] - top))
            total += shrinks[r] * sum_in[r]
        if last:
            share = 1.0 / total
            parts = [part * share for part in parts]
            shrinks[r] = shrinks[r] * share
        else:
            top_out[r] = top
            sum_out[r] = total
        weights.append([part.astype(q_ref.dtype) for part in parts])
    copies = []
    for r in every:
        acc = dot(weights[r][0], value[r], by_key)
        if first:
            acc += dot(weights[r][1].T, cache_ref[r, :KV_RANK], by_width)
            acc += dot(weights[r][2], new_ref[r, :, :KV_RANK], by_key)
        else:
            acc += column(shrinks[r]) * acc_in[r]
        if last:
            stage_ref[r] = acc.astype(out_ref.dtype).reshape(tall // heads, heads, KV_RANK)
            copies.append(
                pltpu.make_async_copy(stage_ref.at[r], out_ref.at[:, r], sems.at[r])
            )
            copies[r].start()
        else:
            acc_out[r] = acc
    for copy in copies:
        copy.wait()


def attend(offsets, bias, wide, own, other, shape, cache, fresh, carry, last):
    rows, tall, width = wide.shape
    steps, heads = shape[0], shape[2]
    first = carry is None
    keys = 2 * own[0].shape[0] * len(offsets)
    state = (
        jax.ShapeDtypeStruct((rows, 1, tall), jnp.float32),
        jax.ShapeDtypeStruct((rows, 1, tall), jnp.float32),
        jax.ShapeDtypeStruct((rows, tall, KV_RANK), jnp.float32),
    )
    final = (steps, rows, heads, KV_RANK)
    operands = (bias, wide, *own, *other, *((cache, fresh) if first else carry))
    vmem, hbm = pl.BlockSpec(memory_space=pltpu.VMEM), pl.BlockSpec(memory_space=pltpu.HBM)
    scratch = []
    if last:
        scratch = [
            pltpu.VMEM((rows, steps, heads, KV_RANK), wide.dtype),
            pltpu.SemaphoreType.DMA((rows,)),
        ]
    return pl.pallas_call(
        functools.partial(attend_kernel, offsets, heads, first, last),
        out_shape=jax.ShapeDtypeStruct(final, wide.dtype) if last else state,
        in_specs=[vmem] * len(operands),
        out_specs=hbm if last else (vmem,) * 3,
        scratch_shapes=scratch,
        cost_estimate=pl.CostEstimate(
            flops=2 * rows * tall * keys * (width + KV_RANK),
            bytes_accessed=2 * rows * (keys + tall) * width,
            transcendentals=rows * tall * keys,
        ),
        compiler_params=pltpu.CompilerParams(vmem_limit_bytes=ATTEND_VMEM),
        name="attend_last" if last else "attend",
    )(*operands)


def spread_exchange(local, assign, row_place, row_count, rows_here):
    group_rows = local.shape[0]
    most_slots = min(rows_here, max(2, 2 * rows_here * SPR // row_count))
    home_group = row_place // SPR
    dest_prompt = assign.reshape(row_count, rows_here)
    in_group = dest_prompt // group_rows == home_group
    rank = jnp.cumsum(in_group.astype(jnp.int32), axis=1) - 1
    slot_ids = jnp.arange(most_slots, dtype=jnp.int32)
    picked = in_group[:, :, None] & (rank[:, :, None] == slot_ids[None, None, :])
    local_id = dest_prompt - home_group * group_rows
    source_index = jnp.sum(jnp.where(picked, local_id[:, :, None], 0), axis=1)
    rows_taken = jnp.take(local, source_index.reshape(-1), axis=0)
    moved = lax.all_to_all(
        rows_taken.reshape((row_count, most_slots) + local.shape[1:]),
        "row",
        split_axis=0,
        concat_axis=0,
        tiled=True,
    )
    owned = lax.dynamic_slice_in_dim(assign, row_place * rows_here, rows_here)
    owned_group = owned // group_rows
    row_ids = jnp.arange(rows_here, dtype=jnp.int32)
    same_before = (owned_group[:, None] == owned_group[None, :]) & (
        row_ids[None, :] < row_ids[:, None]
    )
    own_rank = jnp.sum(same_before.astype(jnp.int32), axis=1)
    flat = moved.reshape((row_count * most_slots,) + local.shape[1:])
    place = row_place % SPR
    chunks = {}
    for offset in ROUNDS:
        index = (owned_group * SPR + partner(offset, place)) * most_slots + own_rank
        taken = jnp.take(flat, index, axis=0)
        chunks[offset] = join_rows([taken[r] for r in range(rows_here)])
    return chunks


def spread_bias(assign, prompt_len, row_ctx, row_place, side, piece, cached):
    rows_here = row_ctx.shape[0]
    owned = lax.dynamic_slice_in_dim(assign, row_place * rows_here, rows_here)
    lives = jnp.take(prompt_len, owned)
    lane = jnp.arange(2 * piece, dtype=jnp.int32)
    spot = jnp.where(lane < piece, side * piece + lane, (1 - side) * piece + lane - piece)
    block = jnp.stack([partner(number, row_place % SPR) for number in ROUNDS])
    spots = (spot[None, :] + block[:, None] * 2 * piece).reshape(1, -1)
    slots = jnp.arange(cached, dtype=jnp.int32)[None, :]
    live = jnp.concatenate([spots < lives[:, None], slots < row_ctx[:, None]], axis=1)
    bias = jnp.where(live, 0.0, -jnp.inf).astype(jnp.float32)
    return jnp.broadcast_to(bias[:, :, None], bias.shape + (LANES,))


def shards(prompt_latent, row_cache, queries, new_latent, prompt_len, assign, row_ctx):
    row_count = lax.axis_size("row")
    rows_here, cached = row_cache.shape[:2]
    local = prompt_latent[0]
    if row_count == SPR:
        packed = pack(SEND_ORDER + (0,), assign, local, rows_here)
        bias = make_bias(assign, prompt_len, row_ctx, local.shape[1], cached)
        mine = {0: packed[0]}
        for offset in SEND_ORDER:
            pairs = [(i, partner(offset, i)) for i in range(row_count)]
            mine[offset] = lax.ppermute(packed[offset], "row", pairs)
    else:
        row_place, side = lax.axis_index("row"), lax.axis_index("tp")
        mine = spread_exchange(local, assign, row_place, row_count, rows_here)
        bias = spread_bias(assign, prompt_len, row_ctx, row_place, side, local.shape[1], cached)
    theirs = {}
    for stage in STAGES:
        for offset in stage:
            theirs[offset] = lax.ppermute(mine[offset], "tp", [(0, 1), (1, 0)])
    fresh = jnp.swapaxes(new_latent, 0, 1)
    wide, turned = spread_queries(queries, jnp.swapaxes(row_cache, 1, 2))
    carry = None
    for number, stage in enumerate(STAGES):
        own, other = [mine[offset] for offset in stage], [theirs[offset] for offset in stage]
        last = number == len(STAGES) - 1
        carry = attend(
            stage, bias, wide, own, other, queries.shape, turned, fresh, carry, last
        )
    return carry


def solution(mesh):
    return jax.shard_map(
        shards,
        mesh=mesh,
        in_specs=(
            P(("group", "row"), None, "tp", None),
            P(("group", "row"), None, None),
            P(None, ("group", "row"), "tp", None),
            P(None, ("group", "row"), None),
            P("group"),
            P("group"),
            P(("group", "row")),
        ),
        out_specs=P(None, ("group", "row"), "tp", None),
        check_vma=False,
    )
```

```python
import functools

import jax
import jax.numpy as jnp
from jax import lax
from jax.experimental import pallas as pl
from jax.experimental.pallas import tpu as pltpu
from jax.sharding import PartitionSpec as P


KV_RANK = 512
ROPE_DIM = 64
NOPE_DIM = 128
SPR = 8
LANES = 128

PACK_VMEM = 4 << 20
ATTEND_VMEM = 16 << 20

SEND_ORDER = (4, 5, 2, 3, 11, 10, 6)
STAGES = ((0,), (4, 5), (2, 3, 11), (10, 6))
ROUNDS = sum(STAGES, ())
MIXED = {10: (7, 1), 11: (1, 7)}


def partner(number, place):
    if number not in MIXED:
        return place ^ number
    inner, outer = MIXED[number]
    middle = ((place >> 1) ^ (place >> 2)) & 1
    return place ^ (middle * inner + (1 - middle) * outer)


def write_bias(bias_ref, lives, caches, place, side, piece):
    block = 2 * piece
    rows, keys, lanes = bias_ref.shape
    slot = lax.broadcasted_iota(jnp.int32, (block, lanes), 0)
    spot = jnp.where(slot < piece, side * piece + slot, (1 - side) * piece + slot - piece)
    kept = lax.broadcasted_iota(jnp.int32, (keys - SPR * block, lanes), 0)
    for r in range(rows):
        for i, number in enumerate(ROUNDS):
            live = spot + partner(number, place) * block < lives[r]
            bias_ref[r, i * block : (i + 1) * block] = jnp.where(live, 0.0, -jnp.inf)
        bias_ref[r, SPR * block :] = jnp.where(kept < caches[r], 0.0, -jnp.inf)


def join_rows(rows):
    return jnp.concatenate(
        [row[:, :KV_RANK] for row in rows] + [row[:, KV_RANK:] for row in rows], axis=1
    )


def pack_kernel(order, rows_here, assign_hbm, latent_hbm, *refs):
    outs, (assign_ref, latent_ref, sems) = refs[: len(order)], refs[len(order) :]
    copies = [
        pltpu.make_async_copy(assign_hbm, assign_ref, sems.at[0]),
        pltpu.make_async_copy(latent_hbm, latent_ref, sems.at[1]),
    ]
    for copy in copies:
        copy.start()
    for copy in copies:
        copy.wait()
    place = lax.axis_index("row")
    for out, offset in zip(outs, order):
        first = partner(offset, place) * rows_here
        out[...] = join_rows([latent_ref[assign_ref[first + r]] for r in range(rows_here)])


def in_hbm(*arrays):
    return [pltpu.with_memory_space_constraint(x, pltpu.HBM) for x in arrays]


def pack(order, assign, local, rows_here):
    _, piece, width = local.shape
    vmem = pl.BlockSpec(memory_space=pltpu.VMEM)
    out = pl.pallas_call(
        functools.partial(pack_kernel, order, rows_here),
        out_shape=[jax.ShapeDtypeStruct((piece, rows_here * width), local.dtype) for _ in order],
        in_specs=[pl.BlockSpec(memory_space=pltpu.HBM)] * 2,
        out_specs=[vmem] * len(order),
        scratch_shapes=[
            pltpu.SMEM(assign.shape, jnp.int32),
            pltpu.VMEM(local.shape, local.dtype),
            pltpu.SemaphoreType.DMA((2,)),
        ],
        compiler_params=pltpu.CompilerParams(vmem_limit_bytes=PACK_VMEM),
        name="pack",
    )(*in_hbm(assign, local))
    return dict(zip(order, out))


def bias_kernel(piece, assign_hbm, length_hbm, ctx_hbm, bias_ref, assign_ref, length_ref, ctx_ref, sems):
    copies = [
        pltpu.make_async_copy(src, dst, sems.at[i])
        for i, (src, dst) in enumerate(
            ((assign_hbm, assign_ref), (length_hbm, length_ref), (ctx_hbm, ctx_ref))
        )
    ]
    for copy in copies:
        copy.start()
    for copy in copies:
        copy.wait()
    rows_here = ctx_hbm.shape[0]
    place, side = lax.axis_index("row"), lax.axis_index("tp")
    lives = [length_ref[assign_ref[place * rows_here + r]] for r in range(rows_here)]
    caches = [ctx_ref[r] for r in range(rows_here)]
    write_bias(bias_ref, lives, caches, place, side, piece)


def make_bias(assign, prompt_len, row_ctx, piece, cached):
    shape = (row_ctx.shape[0], SPR * 2 * piece + cached, LANES)
    return pl.pallas_call(
        functools.partial(bias_kernel, piece),
        out_shape=jax.ShapeDtypeStruct(shape, jnp.float32),
        in_specs=[pl.BlockSpec(memory_space=pltpu.HBM)] * 3,
        out_specs=pl.BlockSpec(memory_space=pltpu.VMEM),
        scratch_shapes=[
            pltpu.SMEM(assign.shape, jnp.int32),
            pltpu.SMEM(prompt_len.shape, jnp.int32),
            pltpu.SMEM(row_ctx.shape, jnp.int32),
            pltpu.SemaphoreType.DMA((3,)),
        ],
        compiler_params=pltpu.CompilerParams(vmem_limit_bytes=PACK_VMEM),
        name="bias",
    )(*in_hbm(assign, prompt_len, row_ctx))


def spread_kernel(q_hbm, cache_hbm, out_ref, cache_ref, q_ref, sems):
    copies = [
        pltpu.make_async_copy(q_hbm, q_ref, sems.at[0]),
        pltpu.make_async_copy(cache_hbm, cache_ref, sems.at[1]),
    ]
    for copy in copies:
        copy.start()
    copies[0].wait()
    steps, rows, heads, width = q_ref.shape
    rope = width - KV_RANK
    for r in range(rows):
        query = q_ref[:, r].reshape(steps * heads, width)
        out_ref[r, :, :KV_RANK] = query[:, :KV_RANK]
        blank = jnp.zeros((steps * heads, rope), query.dtype)
        tail = [query[:, KV_RANK:] if other == r else blank for other in range(rows)]
        out_ref[r, :, KV_RANK:] = jnp.concatenate(tail, axis=1)
    copies[1].wait()


def spread_queries(queries, turned):
    steps, rows, heads, width = queries.shape
    wide = KV_RANK + rows * (width - KV_RANK)
    hbm, vmem = pl.BlockSpec(memory_space=pltpu.HBM), pl.BlockSpec(memory_space=pltpu.VMEM)
    return pl.pallas_call(
        spread_kernel,
        out_shape=[
            jax.ShapeDtypeStruct((rows, steps * heads, wide), queries.dtype),
            jax.ShapeDtypeStruct(turned.shape, turned.dtype),
        ],
        in_specs=[hbm] * 2,
        out_specs=[vmem] * 2,
        scratch_shapes=[
            pltpu.VMEM(queries.shape, queries.dtype),
            pltpu.SemaphoreType.DMA((2,)),
        ],
        compiler_params=pltpu.CompilerParams(vmem_limit_bytes=PACK_VMEM),
        name="spread",
    )(*in_hbm(queries, turned))


def attend_kernel(offsets, heads, first, last, bias_ref, q_ref, *refs):
    refs = list(refs)
    own = [refs.pop(0) for _ in offsets]
    other = [refs.pop(0) for _ in offsets]
    if first:
        cache_ref, new_ref = refs.pop(0), refs.pop(0)
    else:
        top_in, sum_in, acc_in = refs.pop(0), refs.pop(0), refs.pop(0)
    if last:
        out_ref, stage_ref, sems = refs
    else:
        top_out, sum_out, acc_out = refs
    rows, tall, _ = q_ref.shape
    piece = own[0].shape[0]
    block = 2 * piece
    scale = (NOPE_DIM + ROPE_DIM) ** -0.5
    by_width = (((1,), (1,)), ((), ()))
    by_key = (((0,), (0,)), ((), ()))
    dot = functools.partial(lax.dot_general, preferred_element_type=jnp.float32)

    def mask(r, start, count):
        return jnp.concatenate([bias_ref[r, start : start + count]] * (tall // LANES), axis=1)

    def column(line):
        turned = jnp.broadcast_to(line, (LANES, tall)).T
        return jnp.concatenate([turned] * (KV_RANK // LANES), axis=1)

    every = range(rows)
    halves = [half for pair in zip(own, other) for half in pair]
    value = [
        jnp.concatenate([h[:, r * KV_RANK : (r + 1) * KV_RANK] for h in halves], axis=0)
        for r in every
    ]
    rotary = jnp.concatenate([h[:, rows * KV_RANK :] for h in halves], axis=0)
    scores = []
    for r in every:
        found = dot(jnp.concatenate([value[r], rotary], axis=1), q_ref[r], by_width)
        biases = [mask(r, ROUNDS.index(number) * block, block) for number in offsets]
        scores.append([found * scale + jnp.concatenate(biases, axis=0)])
        if first:
            rope = new_ref.shape[2] - KV_RANK
            turn = q_ref[r, :, KV_RANK + r * rope : KV_RANK + (r + 1) * rope]
            narrow = jnp.concatenate([q_ref[r, :, :KV_RANK], turn], axis=1)
            cached = dot(cache_ref[r], narrow, (((0,), (1,)), ((), ())))
            scores[r].append(cached * scale + mask(r, SPR * block, cached.shape[0]))
            fresh = dot(new_ref[r], narrow, by_width)
            step = lax.broadcasted_iota(jnp.int32, fresh.shape, 1) // heads
            slot = lax.broadcasted_iota(jnp.int32, fresh.shape, 0)
            scores[r].append(jnp.where(slot <= step, fresh * scale, -jnp.inf))
    weights, shrinks = [], []
    for r in every:
        tops = [jnp.max(part, axis=0, keepdims=True) for part in scores[r]]
        if not first:
            tops.append(top_in[r])
        top = functools.reduce(jnp.maximum, tops)
        parts = [jnp.exp(part - top) for part in scores[r]]
        total = sum(jnp.sum(part, axis=0, keepdims=True) for part in parts)
        if not first:
            shrinks.append(jnp.exp(top_in[r] - top))
            total += shrinks[r] * sum_in[r]
        if last:
            share = 1.0 / total
            parts = [part * share for part in parts]
            shrinks[r] = shrinks[r] * share
        else:
            top_out[r] = top
            sum_out[r] = total
        weights.append([part.astype(q_ref.dtype) for part in parts])
    copies = []
    for r in every:
        if last:
            shrunk = column(shrinks[r])
            for part in range(tall // LANES):
                here = slice(part * LANES, (part + 1) * LANES)
                acc = dot(weights[r][0][:, here], value[r], by_key)
                acc += shrunk[here] * acc_in[r, here]
                steps = slice(part * LANES // heads, (part + 1) * LANES // heads)
                done = acc.astype(out_ref.dtype)
                stage_ref[r, steps] = done.reshape(LANES // heads, heads, KV_RANK)
                source, target = stage_ref.at[r, steps], out_ref.at[steps, r]
                copies.append(pltpu.make_async_copy(source, target, sems.at[r, part]))
                copies[-1].start()
            continue
        acc = dot(weights[r][0], value[r], by_key)
        if first:
            acc += dot(weights[r][1].T, cache_ref[r, :KV_RANK], by_width)
            acc += dot(weights[r][2], new_ref[r, :, :KV_RANK], by_key)
        else:
            acc += column(shrinks[r]) * acc_in[r]
        acc_out[r] = acc
    for copy in copies:
        copy.wait()


def attend(offsets, bias, wide, own, other, shape, cache, fresh, carry, last):
    rows, tall, width = wide.shape
    steps, heads = shape[0], shape[2]
    first = carry is None
    keys = 2 * own[0].shape[0] * len(offsets)
    state = (
        jax.ShapeDtypeStruct((rows, 1, tall), jnp.float32),
        jax.ShapeDtypeStruct((rows, 1, tall), jnp.float32),
        jax.ShapeDtypeStruct((rows, tall, KV_RANK), jnp.float32),
    )
    final = (steps, rows, heads, KV_RANK)
    operands = (bias, wide, *own, *other, *((cache, fresh) if first else carry))
    vmem, hbm = pl.BlockSpec(memory_space=pltpu.VMEM), pl.BlockSpec(memory_space=pltpu.HBM)
    scratch = []
    if last:
        scratch = [
            pltpu.VMEM((rows, steps, heads, KV_RANK), wide.dtype),
            pltpu.SemaphoreType.DMA((rows, tall // LANES)),
        ]
    return pl.pallas_call(
        functools.partial(attend_kernel, offsets, heads, first, last),
        out_shape=jax.ShapeDtypeStruct(final, wide.dtype) if last else state,
        in_specs=[vmem] * len(operands),
        out_specs=hbm if last else (vmem,) * 3,
        scratch_shapes=scratch,
        cost_estimate=pl.CostEstimate(
            flops=2 * rows * tall * keys * (width + KV_RANK),
            bytes_accessed=2 * rows * (keys + tall) * width,
            transcendentals=rows * tall * keys,
        ),
        compiler_params=pltpu.CompilerParams(vmem_limit_bytes=ATTEND_VMEM),
        name="attend_last" if last else "attend",
    )(*operands)


def spread_exchange(local, assign, row_place, row_count, rows_here):
    group_rows = local.shape[0]
    most_slots = min(rows_here, max(2, 2 * rows_here * SPR // row_count))
    home_group = row_place // SPR
    dest_prompt = assign.reshape(row_count, rows_here)
    in_group = dest_prompt // group_rows == home_group
    rank = jnp.cumsum(in_group.astype(jnp.int32), axis=1) - 1
    slot_ids = jnp.arange(most_slots, dtype=jnp.int32)
    picked = in_group[:, :, None] & (rank[:, :, None] == slot_ids[None, None, :])
    local_id = dest_prompt - home_group * group_rows
    source_index = jnp.sum(jnp.where(picked, local_id[:, :, None], 0), axis=1)
    rows_taken = jnp.take(local, source_index.reshape(-1), axis=0)
    moved = lax.all_to_all(
        rows_taken.reshape((row_count, most_slots) + local.shape[1:]),
        "row",
        split_axis=0,
        concat_axis=0,
        tiled=True,
    )
    owned = lax.dynamic_slice_in_dim(assign, row_place * rows_here, rows_here)
    owned_group = owned // group_rows
    row_ids = jnp.arange(rows_here, dtype=jnp.int32)
    same_before = (owned_group[:, None] == owned_group[None, :]) & (
        row_ids[None, :] < row_ids[:, None]
    )
    own_rank = jnp.sum(same_before.astype(jnp.int32), axis=1)
    flat = moved.reshape((row_count * most_slots,) + local.shape[1:])
    place = row_place % SPR
    chunks = {}
    for offset in ROUNDS:
        index = (owned_group * SPR + partner(offset, place)) * most_slots + own_rank
        taken = jnp.take(flat, index, axis=0)
        chunks[offset] = join_rows([taken[r] for r in range(rows_here)])
    return chunks


def spread_bias(assign, prompt_len, row_ctx, row_place, side, piece, cached):
    rows_here = row_ctx.shape[0]
    owned = lax.dynamic_slice_in_dim(assign, row_place * rows_here, rows_here)
    lives = jnp.take(prompt_len, owned)
    lane = jnp.arange(2 * piece, dtype=jnp.int32)
    spot = jnp.where(lane < piece, side * piece + lane, (1 - side) * piece + lane - piece)
    block = jnp.stack([partner(number, row_place % SPR) for number in ROUNDS])
    spots = (spot[None, :] + block[:, None] * 2 * piece).reshape(1, -1)
    slots = jnp.arange(cached, dtype=jnp.int32)[None, :]
    live = jnp.concatenate([spots < lives[:, None], slots < row_ctx[:, None]], axis=1)
    bias = jnp.where(live, 0.0, -jnp.inf).astype(jnp.float32)
    return jnp.broadcast_to(bias[:, :, None], bias.shape + (LANES,))


def shards(prompt_latent, row_cache, queries, new_latent, prompt_len, assign, row_ctx):
    row_count = lax.axis_size("row")
    rows_here, cached = row_cache.shape[:2]
    local = prompt_latent[0]
    if row_count == SPR:
        packed = pack(SEND_ORDER + (0,), assign, local, rows_here)
        bias = make_bias(assign, prompt_len, row_ctx, local.shape[1], cached)
        mine = {0: packed[0]}
        for offset in SEND_ORDER:
            pairs = [(i, partner(offset, i)) for i in range(row_count)]
            mine[offset] = lax.ppermute(packed[offset], "row", pairs)
    else:
        row_place, side = lax.axis_index("row"), lax.axis_index("tp")
        mine = spread_exchange(local, assign, row_place, row_count, rows_here)
        bias = spread_bias(assign, prompt_len, row_ctx, row_place, side, local.shape[1], cached)
    theirs = {}
    for stage in STAGES:
        for offset in stage:
            theirs[offset] = lax.ppermute(mine[offset], "tp", [(0, 1), (1, 0)])
    fresh = jnp.swapaxes(new_latent, 0, 1)
    wide, turned = spread_queries(queries, jnp.swapaxes(row_cache, 1, 2))
    carry = None
    for number, stage in enumerate(STAGES):
        own, other = [mine[offset] for offset in stage], [theirs[offset] for offset in stage]
        last = number == len(STAGES) - 1
        carry = attend(
            stage, bias, wide, own, other, queries.shape, turned, fresh, carry, last
        )
    return carry


def solution(mesh):
    return jax.shard_map(
        shards,
        mesh=mesh,
        in_specs=(
            P(("group", "row"), None, "tp", None),
            P(("group", "row"), None, None),
            P(None, ("group", "row"), "tp", None),
            P(None, ("group", "row"), None),
            P("group"),
            P("group"),
            P(("group", "row")),
        ),
        out_specs=P(None, ("group", "row"), "tp", None),
        check_vma=False,
    )
```
